32 devices in a mesh: group: 16 (over z, x, core), rep: 2 (over y).
Axes of the slice: x: 2, y: 2, z: 4, core: 2. Of those that a mesh axis runs over, the one named last changes fastest.
Arguments:
- queries: bfloat16 [32, 256, 3072], P(('group', 'rep')), may hold values from -46 to 46
- keys: bfloat16 [32, 256, 3072], P(('group', 'rep')), may hold values from -46 to 46
- values: bfloat16 [32, 256, 3072], P(('group', 'rep')), may hold values from -6 to 6
- grad_output: bfloat16 [32, 256, 3072], P(('group', 'rep')), may hold values from -6 to 6
- weight_codes: bfloat16 [3072, 3072], P('group'), may hold values from -4 to 4
- weight_scales: float32 [3072, 12], P('group'), may hold values from 0.006 to 0.06
Outputs:
- grad_queries: bfloat16 [32, 256, 3072], P(('group', 'rep'))
- grad_keys: bfloat16 [32, 256, 3072], P(('group', 'rep'))
- grad_values: bfloat16 [32, 256, 3072], P(('group', 'rep'))
- grad_weight: float32 [3072, 3072], P(('group', 'rep'))
The draws below stay inside these ranges and needn't reach their ends.
All inputs are finite; a program needn't handle non-finite values.
Results may differ from the reference program's by a relative error of at most 0.029.
Values may be sent and summed in bfloat16 or wider, within the bound.
A program may use at most 128 MiB of HBM per device.

```python
import math
import jax
import jax.numpy as jnp
from jax import lax

H = 24
HD = 128
E = 3072
BLOCK = 256
SEQ = 256
IMG_DEV = 1
ROWS = 3072
IMAGES = 32
N_GROUP = 16
N_REP = 2


def make_pairs(key):
    base = jax.random.fold_in(key, 7)
    key_query, key_keys = jax.random.split(base, 2)
    shape = (IMAGES, SEQ, H, HD)
    query = jnp.clip(jax.random.normal(key_query, shape, jnp.float32), -4.0, 4.0)
    keyset = jnp.clip(jax.random.normal(key_keys, shape, jnp.float32), -4.0, 4.0)
    query = query.reshape(IMAGES, SEQ, H * HD).astype(jnp.bfloat16)
    keyset = keyset.reshape(IMAGES, SEQ, H * HD).astype(jnp.bfloat16)
    return (query, keyset)


def draw_queries(key, part):
    return make_pairs(key)[0]


def draw_keys(key, part):
    return make_pairs(key)[1]


def with_spikes(result, stream_key, source, target, shards_of, factor):
    owner, partner = [(jnp.arange(result.shape[dim]) // (result.shape[dim] // shards_of)).reshape([-1 if axis == dim else 1 for axis in range(result.ndim)]) for dim in (source, target)]
    chosen = jax.random.permutation(stream_key, shards_of)[partner]
    strong = (owner == chosen) | (owner == (partner + shards_of // 2) % shards_of)
    return jnp.where(strong, factor * result, result)


def block_levels(key, extent, shards, low, top_value):
    loudness, own = 1.0, jax.random.fold_in(key, 6)
    for position, shards_of in shards:
        steps = jnp.exp(jax.random.uniform(jax.random.fold_in(own, position), (shards_of,), jnp.float32, low / len(shards), top_value / len(shards)))
        loudness = loudness * jnp.repeat(steps, extent[position] // shards_of).reshape([-1 if axis == position else 1 for axis in range(len(extent))])
    return loudness


def bell_draw(key, dims, deviation, most, shards=(), kind=jnp.bfloat16):
    loudness = block_levels(key, dims, shards, -0.22, 0.18) if shards else 1.0
    entries = jax.random.normal(key, dims, jnp.float32) * deviation * loudness
    return jnp.minimum(jnp.maximum(entries, -most), most).astype(kind)


def bell_draw_with(key, extent, scale, reach, cuts, heavy, dtype=jnp.bfloat16):
    values = scale * jax.random.normal(key, extent, jnp.float32)
    if cuts:
        values = values * block_levels(key, extent, cuts, -0.22, 0.18)
    return jnp.clip(with_spikes(values, jax.random.fold_in(key, 3), *heavy), -reach, reach).astype(dtype)


def setup_inputs(seed: int = 0) -> dict:
    key_of = jax.random.split(jax.random.key(seed), 7)
    return {
        "queries": draw_queries(jax.random.fold_in(key_of[6], 71), 0),
        "keys": draw_keys(jax.random.fold_in(key_of[6], 71), 0),
        "values": bell_draw_with(key_of[2], (IMAGES, SEQ, ROWS), 1.0, 6.0, ((0, 32),), (0, 2, 32, 2.75)),
        "grad_output": bell_draw(key_of[3], (IMAGES, SEQ, E), 1.0, 6.0, ((0, 32),)),
        "weight_codes": bell_draw(key_of[4], (ROWS, E), 1.0, 4.0, ((0, 16),)),
        "weight_scales": jnp.clip(jnp.exp(math.log(0.06) - 2.3025851 * jax.random.uniform(key_of[5], (ROWS, E // BLOCK), jnp.float32) ** block_levels(key_of[5], (ROWS, E // BLOCK), ((0, 16),), -0.2, 0.2)), 0.006, 0.06),
    }


def forward_image(arrays_in):
    query, keyset, valueset = arrays_in
    seq_len = query.shape[0]
    query_heads = query.astype(jnp.float32).reshape(seq_len, H, HD)
    key_heads = keyset.astype(jnp.float32).reshape(seq_len, H, HD)
    value_heads = valueset.astype(jnp.float32).reshape(seq_len, H, HD)
    scores = jnp.einsum("qhd,khd->hqk", query_heads, key_heads) * HD ** -0.5
    highest = jnp.max(scores, axis=2, keepdims=True)
    exponent = jnp.exp(scores - highest)
    probability = exponent / jnp.sum(exponent, axis=2, keepdims=True)
    weight_half = probability.astype(jnp.bfloat16)
    context = jnp.einsum("hqk,khd->qhd", weight_half.astype(jnp.float32), value_heads).astype(jnp.bfloat16)
    return probability, weight_half, context.reshape(seq_len, H * HD)


def context_only(arrays_in):
    return forward_image(arrays_in)[2]


def backward_image(arrays_in):
    query, keyset, valueset, grad_context = arrays_in
    seq_len = query.shape[0]
    probability, weight_half, context = forward_image((query, keyset, valueset))
    query_heads = query.astype(jnp.float32).reshape(seq_len, H, HD)
    key_heads = keyset.astype(jnp.float32).reshape(seq_len, H, HD)
    value_heads = valueset.astype(jnp.float32).reshape(seq_len, H, HD)
    grad_heads = grad_context.astype(jnp.float32).reshape(seq_len, H, HD)
    grad_value = jnp.einsum("hqk,qhd->khd", weight_half.astype(jnp.float32), grad_heads).astype(jnp.bfloat16)
    dprobs = jnp.einsum("qhd,khd->hqk", grad_heads, value_heads)
    row_delta = jnp.sum(probability * dprobs, axis=2, keepdims=True)
    dscores = (probability * (dprobs - row_delta) * HD ** -0.5).astype(jnp.bfloat16).astype(jnp.float32)
    grad_query = jnp.einsum("hqk,khd->qhd", dscores, key_heads).astype(jnp.bfloat16)
    grad_key = jnp.einsum("hqk,qhd->khd", dscores, query_heads).astype(jnp.bfloat16)
    return (grad_query.reshape(seq_len, H * HD), grad_key.reshape(seq_len, H * HD), grad_value.reshape(seq_len, H * HD))


def reference(queries, keys, values, grad_output, weight_codes, weight_scales):
    scaled = weight_codes.astype(jnp.float32).reshape(ROWS, E // BLOCK, BLOCK) * weight_scales[:, :, None]
    weight = scaled.reshape(ROWS, E).astype(jnp.bfloat16)
    contexts = lax.map(context_only, (queries, keys, values))
    grad_flat = jnp.dot(grad_output.reshape(IMAGES * SEQ, E), weight.T, preferred_element_type=jnp.float32)
    grad_context = grad_flat.astype(jnp.bfloat16).reshape(IMAGES, SEQ, ROWS)
    block_total = N_GROUP * N_REP
    context_blocks = contexts.reshape(block_total, IMG_DEV * SEQ, ROWS)
    output_blocks = grad_output.reshape(block_total, IMG_DEV * SEQ, E)

    def add_block(running, pair):
        term = jnp.dot(pair[0].T, pair[1], preferred_element_type=jnp.float32).astype(jnp.bfloat16)
        return running + lax.optimization_barrier(term).astype(jnp.float32), None

    grad_weight, unused = lax.scan(add_block, jnp.zeros((ROWS, E), jnp.float32), (context_blocks, output_blocks))
    grad_queries, grad_keys, grad_values = lax.map(backward_image, (queries, keys, values, grad_context))
    return grad_queries, grad_keys, grad_values, grad_weight
```

```python
import functools
import math

import jax
import jax.numpy as jnp
from jax import lax
from jax.experimental import pallas as pl
from jax.experimental.pallas import tpu as pltpu
from jax.sharding import Mesh, PartitionSpec as P

HD = 128
SCALE = HD ** (-0.5)
CORES = 2


def dot(a, b, dims):
    return lax.dot_general(a, b, (dims, ((), ())), preferred_element_type=jnp.float32)


def probs_t(query, keyset):
    scores = dot(keyset, query, ((1,), (1,)))
    highest = jnp.max(scores, axis=0, keepdims=True)
    exponent = jnp.exp2((scores - highest) * (SCALE * math.log2(math.e)))
    return exponent * (1.0 / jnp.sum(exponent, axis=0, keepdims=True))


def forward_kernel(heads, q_ref, k_ref, v_ref, ctx_ref):
    for head in range(heads):
        cols = slice(head * HD, (head + 1) * HD)
        prob = probs_t(q_ref[:, cols], k_ref[:, cols]).astype(jnp.bfloat16)
        ctx_ref[cols, :] = dot(v_ref[:, cols], prob, ((0,), (0,))).astype(jnp.bfloat16)


def backward_kernel(heads, q_ref, k_ref, v_ref, g_ref, dq_ref, dk_ref, dv_ref):
    for head in range(heads):
        cols = slice(head * HD, (head + 1) * HD)
        query, keyset, grad = q_ref[:, cols], k_ref[:, cols], g_ref[cols, :]
        prob = probs_t(query, keyset)
        dv_ref[:, cols] = dot(prob.astype(jnp.bfloat16), grad, ((1,), (1,))).astype(jnp.bfloat16)
        dprob = dot(v_ref[:, cols], grad, ((1,), (0,)))
        delta = jnp.sum(prob * dprob, axis=0, keepdims=True)
        dscore = (prob * (dprob - delta) * SCALE).astype(jnp.bfloat16)
        dk_ref[:, cols] = dot(dscore, query, ((1,), (0,))).astype(jnp.bfloat16)
        dq_ref[:, cols] = dot(dscore, keyset, ((0,), (0,))).astype(jnp.bfloat16)


def heads_per_step(head_count):
    return next(n for n in (4, 3, 2, 1) if head_count % n == 0)


def forward(query, keyset, valueset):
    seq, rows = query.shape
    heads = heads_per_step(rows // HD)
    wide = pl.BlockSpec((seq, heads * HD), lambda i: (0, i))
    return pl.pallas_call(
        functools.partial(forward_kernel, heads),
        grid=(rows // (heads * HD),),
        in_specs=[wide] * 3,
        out_specs=pl.BlockSpec((heads * HD, seq), lambda i: (i, 0)),
        out_shape=jax.ShapeDtypeStruct((rows, seq), jnp.bfloat16),
        cost_estimate=pl.CostEstimate(
            flops=4 * seq * seq * rows,
            bytes_accessed=8 * seq * rows,
            transcendentals=seq * seq * rows // HD,
        ),
        name="forward",
    )(query, keyset, valueset)


def backward(query, keyset, valueset, grad_t):
    seq, rows = query.shape
    heads = heads_per_step(rows // HD)
    wide = pl.BlockSpec((seq, heads * HD), lambda i: (0, i))
    return pl.pallas_call(
        functools.partial(backward_kernel, heads),
        grid=(rows // (heads * HD),),
        in_specs=[wide] * 3 + [pl.BlockSpec((heads * HD, seq), lambda i: (i, 0))],
        out_specs=[wide] * 3,
        out_shape=[jax.ShapeDtypeStruct((seq, rows), jnp.bfloat16)] * 3,
        cost_estimate=pl.CostEstimate(
            flops=10 * seq * seq * rows,
            bytes_accessed=14 * seq * rows,
            transcendentals=seq * seq * rows // HD,
        ),
        name="backward",
    )(query, keyset, valueset, grad_t)


def term_kernel(count, *refs):
    total = None
    for i in range(count):
        part = dot(refs[i][...], refs[count + i][...], ((1,), (0,)))
        total = part if total is None else total + part
    refs[-1][...] = total.astype(jnp.bfloat16)


def weight_terms(contexts, outputs):
    count = len(contexts)
    rows, seq = contexts[0].shape
    features = outputs[0].shape[1]
    tile = math.gcd(features, 512)
    return pl.pallas_call(
        functools.partial(term_kernel, count),
        grid=(features // tile,),
        in_specs=[pl.BlockSpec((rows, seq), lambda i: (0, 0))] * count
        + [pl.BlockSpec((seq, tile), lambda i: (0, i))] * count,
        out_specs=pl.BlockSpec((rows, tile), lambda i: (0, i)),
        out_shape=jax.ShapeDtypeStruct((rows, features), jnp.bfloat16),
        cost_estimate=pl.CostEstimate(
            flops=2 * rows * seq * features * count,
            bytes_accessed=2 * (count * seq * (rows + features) + rows * features),
            transcendentals=0,
        ),
        name="terms",
    )(*contexts, *outputs)


def restore(codes, scales):
    rows, blocks = scales.shape
    spread = codes.astype(jnp.float32).reshape(rows, blocks, -1) * scales[:, :, None]
    return spread.reshape(rows, -1).astype(jnp.bfloat16)


def per_device(queries, keys, values, grad_output, weight_codes, weight_scales):
    image_count, seq, rows = queries.shape
    features = grad_output.shape[2]
    replicas, spread = lax.axis_size("rep"), lax.axis_size("zx")
    core, rep = lax.axis_index("core"), lax.axis_index("rep")
    slab = rows // (spread * CORES * replicas)
    quarter = spread * slab

    def shifted(value, core_step, rep_step):
        pairs = []
        for c in range(CORES):
            for r in range(replicas):
                to = ((c + core_step) % CORES) * replicas + (r + rep_step) % replicas
                pairs.append((c * replicas + r, to))
        return lax.ppermute(value, ("core", "rep"), pairs)

    codes = lax.dynamic_slice_in_dim(weight_codes, rep * slab, slab, 0)
    scales = lax.dynamic_slice_in_dim(weight_scales, rep * slab, slab, 0)
    weight = lax.all_gather(restore(codes, scales), "zx", axis=0, tiled=True)

    steps = [(c, r) for c in range(CORES) for r in range(replicas)]
    results = []
    total = None
    kept = []
    for image in range(image_count):
        output = grad_output[image]
        outputs = [output] + [shifted(output, 0, r) for r in range(1, replicas)]
        outputs += [shifted(o, 1, 0) for o in outputs]
        context = forward(queries[image], keys[image], values[image])
        context = context.reshape(spread, CORES, replicas, slab, seq)
        contexts = []
        for c, r in steps:
            there = ((core + c) % CORES, (rep + r) % replicas)
            piece = lax.dynamic_slice(
                context, (0, *there, 0, 0), (spread, 1, 1, slab, seq)
            ).reshape(quarter, seq)
            contexts.append(piece if (c, r) == (0, 0) else shifted(piece, c, r))
        kept.append((outputs, contexts))
    terms = weight_terms(
        [c for pair in kept for c in pair[1]], [o for pair in kept for o in pair[0]]
    )
    total = lax.psum_scatter(terms, "zx", scatter_dimension=0, tiled=True)
    for image in range(image_count):
        outputs = kept[image][0]
        grad = jnp.zeros((spread, CORES, replicas, slab, seq), jnp.bfloat16)
        for (c, r), output in zip(steps, outputs):
            piece = dot(weight, output, ((1,), (1,))).astype(jnp.bfloat16)
            if (c, r) != (0, 0):
                piece = shifted(piece, -c, -r)
            there = ((core + c) % CORES, (rep + r) % replicas)
            grad = lax.dynamic_update_slice(
                grad, piece.reshape(spread, 1, 1, slab, seq), (0, *there, 0, 0)
            )
        results.append(
            backward(queries[image], keys[image], values[image], grad.reshape(rows, seq))
        )
    grads = [
        parts[0][None] if image_count == 1 else jnp.stack(parts) for parts in zip(*results)
    ]
    return (*grads, total.astype(jnp.float32))


def solution(mesh):
    groups, replicas = mesh.shape["group"], mesh.shape["rep"]
    split = Mesh(
        mesh.devices.reshape(groups // CORES, CORES, replicas), ("zx", "core", "rep")
    )
    images = P(("zx", "core", "rep"), None, None)
    shards = P(("zx", "core"), None)
    return jax.shard_map(
        per_device,
        mesh=split,
        in_specs=(images,) * 4 + (shards,) * 2,
        out_specs=(images,) * 3 + (P(("zx", "core", "rep"), None),),
        check_vma=False,
    )
```

```python
import functools
import itertools
import math

import jax
import jax.numpy as jnp
from jax import lax
from jax.experimental import pallas as pl
from jax.experimental.pallas import tpu as pltpu
from jax.sharding import Mesh, PartitionSpec as P

HD = 128
SCALE = HD ** (-0.5)
CORES = 2
PLANE = ("x", "core", "rep")


def dot(a, b, dims):
    return lax.dot_general(a, b, (dims, ((), ())), preferred_element_type=jnp.float32)


def probs_t(query, keyset):
    scores = dot(keyset, query, ((1,), (1,)))
    highest = jnp.max(scores, axis=0, keepdims=True)
    exponent = jnp.exp2((scores - highest) * (SCALE * math.log2(math.e)))
    return exponent * (1.0 / jnp.sum(exponent, axis=0, keepdims=True))


def forward_kernel(heads, q_ref, k_ref, v_ref, ctx_ref):
    for head in range(heads):
        cols = slice(head * HD, (head + 1) * HD)
        prob = probs_t(q_ref[:, cols], k_ref[:, cols]).astype(jnp.bfloat16)
        ctx_ref[cols, :] = dot(v_ref[:, cols], prob, ((0,), (0,))).astype(jnp.bfloat16)


def backward_kernel(heads, q_ref, k_ref, v_ref, g_ref, dq_ref, dk_ref, dv_ref):
    for head in range(heads):
        cols = slice(head * HD, (head + 1) * HD)
        query, keyset, grad = q_ref[:, cols], k_ref[:, cols], g_ref[cols, :]
        prob = probs_t(query, keyset)
        dv_ref[:, cols] = dot(prob.astype(jnp.bfloat16), grad, ((1,), (1,))).astype(jnp.bfloat16)
        dprob = dot(v_ref[:, cols], grad, ((1,), (0,)))
        delta = jnp.sum(prob * dprob, axis=0, keepdims=True)
        dscore = (prob * (dprob - delta) * SCALE).astype(jnp.bfloat16)
        dk_ref[:, cols] = dot(dscore, query, ((1,), (0,))).astype(jnp.bfloat16)
        dq_ref[:, cols] = dot(dscore, keyset, ((0,), (0,))).astype(jnp.bfloat16)


def heads_per_step(head_count):
    return next(n for n in (4, 3, 2, 1) if head_count % n == 0)


def forward(query, keyset, valueset):
    seq, rows = query.shape
    heads = heads_per_step(rows // HD)
    wide = pl.BlockSpec((seq, heads * HD), lambda i: (0, i))
    return pl.pallas_call(
        functools.partial(forward_kernel, heads),
        grid=(rows // (heads * HD),),
        in_specs=[wide] * 3,
        out_specs=pl.BlockSpec((heads * HD, seq), lambda i: (i, 0)),
        out_shape=jax.ShapeDtypeStruct((rows, seq), jnp.bfloat16),
        cost_estimate=pl.CostEstimate(
            flops=4 * seq * seq * rows,
            bytes_accessed=8 * seq * rows,
            transcendentals=seq * seq * rows // HD,
        ),
        name="forward",
    )(query, keyset, valueset)


def backward(query, keyset, valueset, grad_t):
    seq, rows = query.shape
    heads = heads_per_step(rows // HD)
    wide = pl.BlockSpec((seq, heads * HD), lambda i: (0, i))
    return pl.pallas_call(
        functools.partial(backward_kernel, heads),
        grid=(rows // (heads * HD),),
        in_specs=[wide] * 3 + [pl.BlockSpec((heads * HD, seq), lambda i: (i, 0))],
        out_specs=[wide] * 3,
        out_shape=[jax.ShapeDtypeStruct((seq, rows), jnp.bfloat16)] * 3,
        cost_estimate=pl.CostEstimate(
            flops=10 * seq * seq * rows,
            bytes_accessed=14 * seq * rows,
            transcendentals=seq * seq * rows // HD,
        ),
        name="backward",
    )(query, keyset, valueset, grad_t)


def term_kernel(count, *refs):
    total = None
    for i in range(count):
        part = dot(refs[i][...], refs[count + i][...], ((1,), (0,)))
        total = part if total is None else total + part
    refs[-1][...] = total.astype(jnp.bfloat16)


def weight_terms(contexts, outputs):
    count = len(contexts)
    rows, seq = contexts[0].shape
    features = outputs[0].shape[1]
    tile = math.gcd(features, 512)
    return pl.pallas_call(
        functools.partial(term_kernel, count),
        grid=(features // tile,),
        in_specs=[pl.BlockSpec((rows, seq), lambda i: (0, 0))] * count
        + [pl.BlockSpec((seq, tile), lambda i: (0, i))] * count,
        out_specs=pl.BlockSpec((rows, tile), lambda i: (0, i)),
        out_shape=jax.ShapeDtypeStruct((rows, features), jnp.bfloat16),
        cost_estimate=pl.CostEstimate(
            flops=2 * rows * seq * features * count,
            bytes_accessed=2 * (count * seq * (rows + features) + rows * features),
            transcendentals=0,
        ),
        name="terms",
    )(*contexts, *outputs)


def restore(codes, scales):
    rows, blocks = scales.shape
    spread = codes.astype(jnp.float32).reshape(rows, blocks, -1) * scales[:, :, None]
    return spread.reshape(rows, -1).astype(jnp.bfloat16)


def per_device(queries, keys, values, grad_output, weight_codes, weight_scales):
    image_count, seq, rows = queries.shape
    depth = lax.axis_size("z")
    extents = tuple(lax.axis_size(axis) for axis in PLANE)
    home = tuple(lax.axis_index(axis) for axis in PLANE)
    replicas, peers = extents[-1], math.prod(extents)
    slab = rows // (depth * peers)
    share = depth * slab
    steps = list(itertools.product(*(range(n) for n in extents)))

    def shifted(value, step):
        pairs = []
        for source, place in enumerate(steps):
            to = 0
            for at, move, n in zip(place, step, extents):
                to = to * n + (at + move) % n
            pairs.append((source, to))
        return lax.ppermute(value, PLANE, pairs)

    def start_at(step):
        return (0, *((h + s) % n for h, s, n in zip(home, step, extents)), 0, 0)

    own = home[-1] * slab
    codes = lax.dynamic_slice_in_dim(weight_codes, own, slab, 0)
    scales = lax.dynamic_slice_in_dim(weight_scales, own, slab, 0)
    weight = lax.all_gather(restore(codes, scales), "z", axis=0, tiled=True)

    kept = []
    for image in range(image_count):
        first = grad_output[image]
        straight = [shifted(first, (0, 0, r)) for r in range(1, replicas)]
        across = shifted(first, (1, 0, 0))
        context = forward(queries[image], keys[image], values[image])
        context = context.reshape(depth, *extents, slab, seq)
        pieces = [
            lax.dynamic_slice(context, start_at(step), (depth, 1, 1, 1, slab, seq)).reshape(
                share, seq
            )
            for step in steps
        ]
        contexts = [pieces[0]] + [shifted(p, step) for p, step in zip(pieces[1:], steps[1:])]
        across, straight, _ = lax.optimization_barrier((across, straight, pieces[0]))
        half = seq // 2
        corner = [
            jnp.concatenate(
                [shifted(piece[:half], (1, 0, 0)), shifted(across[half:], (0, 0, r))]
            )
            for r, piece in enumerate(straight, 1)
        ]
        near = {(0, 0): first, (1, 0): across}
        for r in range(1, replicas):
            near[0, r], near[1, r] = straight[r - 1], corner[r - 1]
        outputs = [
            near[x, r] if c == 0 else shifted(near[x, r], (0, 1, 0)) for x, c, r in steps
        ]
        kept.append((outputs, contexts))
    terms = weight_terms(
        [c for pair in kept for c in pair[1]], [o for pair in kept for o in pair[0]]
    )
    total = lax.psum_scatter(terms, "z", scatter_dimension=0, tiled=True)
    results = []
    for image in range(image_count):
        grad = jnp.zeros((depth, *extents, slab, seq), jnp.bfloat16)
        for step, output in zip(steps, kept[image][0]):
            piece = dot(weight, output, ((1,), (1,))).astype(jnp.bfloat16)
            if any(step):
                piece = shifted(piece, tuple(-s for s in step))
            grad = lax.dynamic_update_slice(
                grad, piece.reshape(depth, 1, 1, 1, slab, seq), start_at(step)
            )
        results.append(
            backward(queries[image], keys[image], values[image], grad.reshape(rows, seq))
        )
    grads = [
        parts[0][None] if image_count == 1 else jnp.stack(parts) for parts in zip(*results)
    ]
    return (*grads, total.astype(jnp.float32))


def solution(mesh):
    groups, replicas = mesh.shape["group"], mesh.shape["rep"]
    split = Mesh(
        mesh.devices.reshape(groups // (2 * CORES), 2, CORES, replicas), ("z", *PLANE)
    )
    images = P(("z", *PLANE), None, None)
    shards = P(("z", "x", "core"), None)
    return jax.shard_map(
        per_device,
        mesh=split,
        in_specs=(images,) * 4 + (shards,) * 2,
        out_specs=(images,) * 3 + (P(("z", *PLANE), None),),
        check_vma=False,
    )
```
